32 devices in a mesh: ctx: 8 (over z, y), tensor: 4 (over x, core).
Axes of the slice: x: 2, y: 2, z: 4, core: 2. Of those that a mesh axis runs over, the one named last changes fastest.
Arguments:
- hidden_in: bfloat16 [1, 1024, 2048], P(None, 'ctx', 'tensor'), may hold values from -6 to 6
- out_grad: bfloat16 [1, 1024, 2048], P(None, 'ctx', 'tensor'), may hold values from -6 to 6
- segment_ids: int32 [1, 1024], replicated, may hold values from 0 to 4, never falling along the last dimension, each value on 1 to 512 neighbouring positions
- adapter_pick: int32 [1], replicated, may hold values from 0 to 7
- norm_gains: float32 [2, 2048], replicated, may hold values from 0.5 to 1.5
- head_gain: float32 [256], replicated, may hold values from 0.5 to 1.5
- mixer_in: bfloat16 [2048, 16, 768], P('ctx', 'tensor'), may hold values from -0.125 to 0.125
- rate_in: bfloat16 [2048, 16, 2], P('ctx', 'tensor'), may hold values from -0.125 to 0.125
- kernel_taps: bfloat16 [4, 16, 512], P(None, 'tensor'), may hold values from -3 to 3
- decay_scale: float32 [16], P('tensor'), may hold values from 0.004 to 0.08
- decay_bias: float32 [16], P('tensor'), may hold values from -2 to 1
- mixer_out: bfloat16 [16, 256, 2048], P('tensor', None, 'ctx'), may hold values from -0.1875 to 0.1875
- expand_in: bfloat16 [2048, 2, 5632], P('ctx', None, 'tensor'), may hold values from -0.125 to 0.125
- expand_out: bfloat16 [5632, 2048], P('tensor', 'ctx'), may hold values from -0.078125 to 0.078125
- adapter_down: bfloat16 [8, 128, 2048], P(None, None, 'ctx'), may hold values from -0.125 to 0.125
- adapter_back: bfloat16 [8, 32, 2048], P(None, None, 'ctx'), may hold values from -0.75 to 0.75
- adapter_keys: bfloat16 [8, 2, 16, 2048], P(None, None, None, 'tensor'), may hold values from -0.75 to 0.75
- adapter_values: bfloat16 [8, 2, 16, 4096], P(None, None, None, 'tensor'), may hold values from -0.75 to 0.75
- adapter_rates: bfloat16 [8, 2, 16, 16], P(None, None, None, 'tensor'), may hold values from -0.75 to 0.75
- adapter_expand: bfloat16 [8, 2, 16, 5632], P(None, None, None, 'tensor'), may hold values from -0.75 to 0.75
- adapter_mixer: bfloat16 [8, 16, 4096], P(None, None, 'tensor'), may hold values from -0.09375 to 0.09375
- adapter_hidden: bfloat16 [8, 16, 5632], P(None, None, 'tensor'), may hold values from -0.078125 to 0.078125
Outputs:
- hidden_out: bfloat16 [1, 1024, 2048], P(None, 'ctx', 'tensor')
- input_grad: float32 [1, 1024, 2048], P(None, 'ctx', 'tensor')
- grad_down: float32 [8, 128, 2048], P(None, None, ('ctx', 'tensor'))
- grad_back: float32 [8, 32, 2048], P(None, None, ('ctx', 'tensor'))
- grad_keys: float32 [8, 2, 16, 2048], P(None, None, None, 'tensor')
- grad_values: float32 [8, 2, 16, 4096], P(None, None, None, 'tensor')
- grad_rates: float32 [8, 2, 16, 16], P(None, None, None, 'tensor')
- grad_expand: float32 [8, 2, 16, 5632], P(None, None, None, 'tensor')
- grad_mixer: float32 [8, 16, 4096], P(None, None, 'tensor')
- grad_hidden: float32 [8, 16, 5632], P(None, None, 'tensor')
The draws below stay inside these ranges and needn't reach their ends.
Inputs may be any that keep to these rules, and one draw needn't show every extreme that they name: `segment_ids`: along each sequence the ids never fall; every document has 1 to 512 tokens and one has exactly 512.
All inputs are finite; a program needn't handle non-finite values.
Results may differ from the reference program's by a relative error of at most 0.022.
Values may be sent and summed in bfloat16 or wider, within the bound.
No kernel may reach another device: no remote copies, remote signals or barrier semaphores. Data moves between devices by JAX's collectives and lax.ppermute only.
A program may use at most 192 MiB of HBM per device.

```python
import math
import jax
import jax.numpy as jnp
import numpy as np
from jax import lax

D = 2048
HEADS = 16
DK = 128
DV = 256
FF = 5632
CONV = 4
BLOCK = 64
FACTOR_INNER_DIM = 16
ADAPT = 8
SEQS = 1
LEN = 1024
DOC_MOST = 512


def shard_levels(key, extent, split, low, high):
    factor_of = 1.0
    for dim, shards_of in split:
        heights = jax.random.uniform(jax.random.fold_in(jax.random.fold_in(key, 6), dim), (shards_of,), jnp.float32, low / len(split), high / len(split))
        factor_of = factor_of * jnp.repeat(jnp.exp(heights), extent[dim] // shards_of).reshape((-1,) + (1,) * (len(extent) - 1 - dim))
    return factor_of


def length_profile(number_of, total, most, skew):
    loads = [(1 << 20) // math.isqrt(rank ** skew) + 1 for rank in range(2, number_of + 1)]
    spare, holding = total - most - (number_of - 1), [1] * (number_of - 1)
    while spare > 0:
        free = [i for i in range(number_of - 1) if holding[i] < most]
        pool, remaining = sum([loads[i] for i in free]), spare
        for i in free:
            more = min(most - holding[i], max(1, remaining * loads[i] // pool), spare)
            holding[i] = holding[i] + more
            spare = spare - more
    return np.array([most] + holding)


def ragged_sizes(stream_key, number_of, total, most, skew):
    if number_of == 2:
        one = jax.random.randint(stream_key, (), max(1, total - most), min(most, total - 1) + 1)
        return jnp.stack([one, total - one])
    sizes = jnp.asarray(length_profile(number_of, total, most, skew), jnp.int32)
    twos = (number_of - 1) // 2
    donor, sink = sizes[1:1 + 2 * twos:2], sizes[2:2 + 2 * twos:2]
    margin = jnp.minimum(donor - 1, most - sink)
    passed = jax.random.randint(jax.random.fold_in(stream_key, 1), (twos,), 0, 1 << 20) % (margin + 1)
    sizes = sizes.at[1:1 + 2 * twos:2].set(donor - passed).at[2:2 + 2 * twos:2].set(sink + passed)
    return sizes[jax.random.permutation(jax.random.fold_in(stream_key, 2), number_of)]


def scatter_about(stream_key, shape, scale, bound, shards=(), kind=jnp.bfloat16):
    values = jax.random.normal(stream_key, shape, jnp.float32) * scale
    if len(shards) > 0:
        values = shard_levels(stream_key, shape, shards, -0.22, 0.18) * values
    return jnp.clip(values, min=-bound, max=bound).astype(kind)


def setup_inputs(seed: int = 0) -> dict:
    keys = jax.random.split(jax.random.key(seed), 23)
    hidden_in = scatter_about(keys[0], (SEQS, LEN, D), 1.0, 6.0, ((1, 8), (2, 4)))
    out_grad = scatter_about(keys[1], (SEQS, LEN, D), 1.0, 6.0, ((1, 8), (2, 4)))
    segment_ids = jax.vmap(lambda own: jnp.searchsorted(jnp.cumsum(ragged_sizes(own, 2 * LEN // DOC_MOST + 1, LEN, DOC_MOST, 0)), jnp.arange(LEN), side="right"))(jax.random.split(keys[2], SEQS)).reshape((SEQS, LEN)).astype(jnp.int32)
    adapter_pick = jax.random.randint(keys[3], (SEQS,), 0, ADAPT).astype(jnp.int32)
    norm_gains = jnp.clip(1.0 + 0.1 * jax.random.normal(keys[4], (2, D), jnp.float32), 0.5, 1.5)
    head_gain = jnp.clip(1.0 + 0.1 * jax.random.normal(keys[5], (DV,), jnp.float32), 0.5, 1.5)
    mixer_in = scatter_about(keys[6], (D, HEADS, 2 * DK + 2 * DV), D ** -0.5, 0.125, ((0, 8), (1, 4)))
    rate_in = scatter_about(keys[7], (D, HEADS, 2), D ** -0.5, 0.125, ((0, 8), (1, 4)))
    kernel_taps = scatter_about(keys[8], (CONV, HEADS, 2 * DK + DV), 0.5, 3.0, ((1, 4),))
    decay_scale = jnp.clip(jnp.exp(math.log(0.08) - 2.9957322 * jax.random.uniform(keys[9], (HEADS,), jnp.float32) ** shard_levels(keys[9], (HEADS,), ((0, 4),), -0.2, 0.2)), 0.004, 0.08)
    decay_bias = jnp.clip(-2.0 + 3.0 * jax.random.uniform(keys[10], (HEADS,), jnp.float32) ** shard_levels(keys[10], (HEADS,), ((0, 4),), -0.2, 0.2), -2.0, 1.0)
    mixer_out = scatter_about(keys[11], (HEADS, DV, D), (HEADS * DV // 4) ** -0.5, 0.1875, ((0, 4), (2, 8)))
    expand_in = scatter_about(keys[12], (D, 2, FF), D ** -0.5, 0.125, ((0, 8), (2, 4)))
    expand_out = scatter_about(keys[13], (FF, D), FF ** -0.5, 0.078125, ((0, 4), (1, 8)))
    adapter_down = scatter_about(keys[14], (ADAPT, 8 * FACTOR_INNER_DIM, D), D ** -0.5, 0.125, ((2, 8),))
    adapter_back = scatter_about(keys[15], (ADAPT, 2 * FACTOR_INNER_DIM, D), (4 * FACTOR_INNER_DIM) ** -0.5, 0.75, ((2, 8),))
    adapter_keys = scatter_about(keys[16], (ADAPT, 2, FACTOR_INNER_DIM, HEADS * DK), (4 * FACTOR_INNER_DIM) ** -0.5, 0.75, ((3, 4),))
    adapter_values = scatter_about(keys[17], (ADAPT, 2, FACTOR_INNER_DIM, HEADS * DV), (4 * FACTOR_INNER_DIM) ** -0.5, 0.75, ((3, 4),))
    adapter_rates = scatter_about(keys[18], (ADAPT, 2, FACTOR_INNER_DIM, HEADS), (4 * FACTOR_INNER_DIM) ** -0.5, 0.75, ((3, 4),))
    adapter_expand = scatter_about(keys[19], (ADAPT, 2, FACTOR_INNER_DIM, FF), (4 * FACTOR_INNER_DIM) ** -0.5, 0.75, ((3, 4),))
    adapter_mixer = scatter_about(keys[20], (ADAPT, FACTOR_INNER_DIM, HEADS * DV), (HEADS * DV) ** -0.5, 0.09375, ((2, 4),))
    adapter_hidden = scatter_about(keys[21], (ADAPT, FACTOR_INNER_DIM, FF), FF ** -0.5, 0.078125, ((2, 4),))
    return {"hidden_in": hidden_in, "out_grad": out_grad, "segment_ids": segment_ids, "adapter_pick": adapter_pick, "norm_gains": norm_gains, "head_gain": head_gain, "mixer_in": mixer_in, "rate_in": rate_in, "kernel_taps": kernel_taps, "decay_scale": decay_scale, "decay_bias": decay_bias, "mixer_out": mixer_out, "expand_in": expand_in, "expand_out": expand_out, "adapter_down": adapter_down, "adapter_back": adapter_back, "adapter_keys": adapter_keys, "adapter_values": adapter_values, "adapter_rates": adapter_rates, "adapter_expand": adapter_expand, "adapter_mixer": adapter_mixer, "adapter_hidden": adapter_hidden}


accurate_matrix_product = lax.Precision.HIGHEST

@jax.custom_vjp
def low(v):
    return lax.optimization_barrier(v.astype(jnp.bfloat16)).astype(jnp.float32)

@jax.custom_vjp
def thin_factor_pullback(v):
    return v

def low_keep(v):
    return (low(v), None)

def low_pass(kept, grad):
    return (grad,)

def back_keep(v):
    return (v, None)

def back_low(kept, grad):
    return (low(grad),)
low.defvjp(low_keep, low_pass)
thin_factor_pullback.defvjp(back_keep, back_low)

def rms_scale(value):
    return value * lax.rsqrt(lax.optimization_barrier(jnp.mean(value * value, axis=-1, keepdims=True)) + 1e-06)

def unit_rows(value):
    return value * lax.rsqrt(lax.optimization_barrier(jnp.sum(value * value, axis=-1, keepdims=True)) + 1e-06)

def swish(value):
    return value * jax.nn.sigmoid(value)

def prepare_heads(padded, rates, labels_pad, taps, decay_scale, decay_bias):
    width = rates.shape[-3]
    reach = taps.shape[0]
    lead = reach - 1
    current = labels_pad[..., lead:]
    mixed = jnp.zeros(padded.shape[:-3] + (width,) + padded.shape[-2:], jnp.float32)
    for shift_by in range(reach):
        earlier = labels_pad[..., lead - shift_by:lead - shift_by + width]
        keep = jnp.where(earlier == current, 1.0, 0.0)[..., None, None]
        mixed = mixed + taps[shift_by] * padded[..., lead - shift_by:lead - shift_by + width, :, :] * keep
    active = swish(mixed)
    query = unit_rows(active[..., :DK]) * DK ** (-0.5)
    key = unit_rows(active[..., DK:2 * DK])
    value = active[..., 2 * DK:]
    beta = jax.nn.sigmoid(rates[..., 1])
    log_decay = -decay_scale * jax.nn.softplus(rates[..., 0] + decay_bias)
    return (query, key, value, beta, log_decay)

def finish_heads(mixed, gate, head_gain):
    normed = mixed * lax.rsqrt(lax.optimization_barrier(jnp.mean(mixed * mixed, axis=-1, keepdims=True)) + 1e-05)
    return normed * head_gain * swish(gate)

def unit_inverse(coupling):
    size = coupling.shape[-1]
    identity = jnp.eye(size, dtype=coupling.dtype)
    power = coupling
    result = identity - coupling
    for level in range((size - 1).bit_length() - 1):
        power = jnp.einsum('hij,hjk->hik', power, power, precision=accurate_matrix_product)
        result = result + jnp.einsum('hij,hjk->hik', result, power, precision=accurate_matrix_product)
    return result

def block_parts(key, beta, log_decay, labels, label_before):
    size = labels.shape[-1]
    cumulative = jnp.cumsum(log_decay, axis=-1)
    row_index = lax.broadcasted_iota(jnp.int32, (size, size), 0)
    column_index = lax.broadcasted_iota(jnp.int32, (size, size), 1)
    linked = (labels[:, None] == labels[None, :]) & (row_index >= column_index)
    spread = jnp.where(linked[None], cumulative[:, :, None] - cumulative[:, None, :], 0.0)
    decay = jnp.where(linked[None], jnp.exp(spread), 0.0)
    strict = jnp.where((row_index > column_index)[None], decay, 0.0)
    carry_in = jnp.where(labels[None, :] == label_before, jnp.exp(cumulative), 0.0)
    coupling = beta[:, :, None] * jnp.einsum('hik,hjk->hij', key, key, precision=accurate_matrix_product) * strict
    return (decay, carry_in, unit_inverse(coupling))

def block_step(state, block):
    query, key, value, beta, log_decay, labels, label_before = block
    decay, carry_in, inverse = block_parts(key, beta, log_decay, labels, label_before)
    weights_key = jnp.einsum('hij,hjk->hik', inverse, (beta * carry_in)[:, :, None] * key, precision=accurate_matrix_product)
    targets = jnp.einsum('hij,hjv->hiv', inverse, beta[:, :, None] * value, precision=accurate_matrix_product)
    fresh = targets - jnp.einsum('hck,hvk->hcv', weights_key, state, precision=accurate_matrix_product)
    scores = jnp.einsum('hik,hjk->hij', query, key, precision=accurate_matrix_product) * decay
    output = carry_in[:, :, None] * jnp.einsum('hck,hvk->hcv', query, state, precision=accurate_matrix_product)
    output = output + jnp.einsum('hij,hjv->hiv', scores, fresh, precision=accurate_matrix_product)
    tail = decay[:, -1, :]
    new_state = carry_in[:, -1][:, None, None] * state
    new_state = new_state + jnp.einsum('hjv,hjk->hvk', fresh * tail[:, :, None], key, precision=accurate_matrix_product)
    return (new_state, output)

def split_blocks(query, key, value, beta, log_decay, labels, label_before):
    heads = key.shape[0]
    count = key.shape[1] // BLOCK

    def cut(array):
        shaped = array.reshape((heads, count, BLOCK) + array.shape[2:])
        return jnp.moveaxis(shaped, 1, 0)
    label_blocks = labels.reshape(count, BLOCK)
    befores = jnp.concatenate([jnp.reshape(label_before, (1,)), label_blocks[:-1, -1]])
    return (cut(query), cut(key), cut(value), cut(beta), cut(log_decay), label_blocks, befores)

def run_piece(state, query, key, value, beta, log_decay, labels, label_before):
    blocks = split_blocks(query, key, value, beta, log_decay, labels, label_before)
    final, outputs = lax.scan(jax.checkpoint(block_step), state, blocks)
    heads = query.shape[0]
    return (final, jnp.moveaxis(outputs, 0, 1).reshape(heads, -1, outputs.shape[-1]))

def forward(resid_in, tables, weights, labels, pick):
    norm_gains, head_gain, mixer_in, rate_in, taps, decay_scale, decay_bias, mixer_out, expand_in, expand_out = weights
    table_down, table_back, table_keys, table_values, table_rates, table_expand, table_mixer, table_hidden = tables
    down = table_down[pick]
    back = table_back[pick]
    keys_sel = table_keys[pick]
    values_sel = table_values[pick]
    rates_sel = table_rates[pick]
    widen_chosen_factor = table_expand[pick]
    mixer_sel = table_mixer[pick]
    hidden_sel = table_hidden[pick]
    token_count_per_doc = resid_in.shape[0]
    heads = mixer_in.shape[1]
    qkv_width = 2 * DK + DV
    lead = taps.shape[0] - 1
    first_norm = low(rms_scale(resid_in) * norm_gains[0])
    low_mix = jnp.dot(first_norm, down[:6 * FACTOR_INNER_DIM].T, precision=accurate_matrix_product)
    base = jnp.einsum('ld,dhc->lhc', first_norm, mixer_in, precision=accurate_matrix_product)
    rate_base = jnp.einsum('ld,dhc->lhc', first_norm, rate_in, precision=accurate_matrix_product)
    added_keys = jnp.einsum('lxr,xrn->lxn', low_mix[:, :2 * FACTOR_INNER_DIM].reshape(token_count_per_doc, 2, FACTOR_INNER_DIM), keys_sel, precision=accurate_matrix_product)
    added_keys = jnp.moveaxis(added_keys.reshape(token_count_per_doc, 2, heads, DK), 1, 2).reshape(token_count_per_doc, heads, 2 * DK)
    added_values = jnp.einsum('lxr,xrn->lxn', low_mix[:, 2 * FACTOR_INNER_DIM:4 * FACTOR_INNER_DIM].reshape(token_count_per_doc, 2, FACTOR_INNER_DIM), values_sel, precision=accurate_matrix_product)
    added_values = added_values.reshape(token_count_per_doc, 2, heads, DV)
    added_rates = jnp.einsum('lxr,xrh->lxh', low_mix[:, 4 * FACTOR_INNER_DIM:].reshape(token_count_per_doc, 2, FACTOR_INNER_DIM), rates_sel, precision=accurate_matrix_product)
    added_rates = jnp.moveaxis(added_rates, 1, 2)
    pre_qkv = thin_factor_pullback(low(base[..., :qkv_width] + jnp.concatenate([added_keys, added_values[:, 0]], axis=-1)))
    gate = thin_factor_pullback(base[..., qkv_width:] + added_values[:, 1])
    rates = thin_factor_pullback(rate_base + added_rates)
    padded = jnp.concatenate([jnp.zeros((lead, heads, qkv_width), jnp.float32), pre_qkv], axis=0)
    labels_pad = jnp.concatenate([jnp.full((lead,), -1, jnp.int32), labels])
    fields = prepare_heads(padded, rates, labels_pad, taps, decay_scale, decay_bias)
    fields = tuple((jnp.moveaxis(field, 1, 0) for field in fields))
    start = jnp.zeros((heads, DV, DK), jnp.float32)
    final, mixed = run_piece(start, fields[0], fields[1], fields[2], fields[3], fields[4], labels, jnp.array(-1, jnp.int32))
    attended = low(finish_heads(jnp.moveaxis(mixed, 0, 1), gate, head_gain))
    flat = attended.reshape(token_count_per_doc, heads * DV)
    low_out = jnp.dot(flat, mixer_sel.T, precision=accurate_matrix_product)
    branch = jnp.einsum('lhv,hvd->ld', attended, mixer_out, precision=accurate_matrix_product) + jnp.dot(low_out, back[:FACTOR_INNER_DIM], precision=accurate_matrix_product)
    resid_mid = resid_in + thin_factor_pullback(branch)
    second_norm = low(rms_scale(resid_mid) * norm_gains[1])
    thin_factor_dense_block = jnp.dot(second_norm, down[6 * FACTOR_INNER_DIM:].T, precision=accurate_matrix_product)
    gating_lift_matrix = jnp.einsum('ld,dcf->lcf', second_norm, expand_in, precision=accurate_matrix_product)
    gating_lift_matrix = thin_factor_pullback(gating_lift_matrix + jnp.einsum('fzu,zuv->fzv', thin_factor_dense_block.reshape(token_count_per_doc, 2, FACTOR_INNER_DIM), widen_chosen_factor, precision=accurate_matrix_product))
    hidden_act = low(swish(gating_lift_matrix[:, 0]) * gating_lift_matrix[:, 1])
    low_hid = jnp.dot(hidden_act, hidden_sel.T, precision=accurate_matrix_product)
    ffn_part = jnp.dot(hidden_act, expand_out, precision=accurate_matrix_product) + jnp.dot(low_hid, back[FACTOR_INNER_DIM:], precision=accurate_matrix_product)
    return resid_mid + thin_factor_pullback(ffn_part)

def reference(hidden_in, out_grad, segment_ids, adapter_pick, norm_gains, head_gain, mixer_in, rate_in, kernel_taps, decay_scale, decay_bias, mixer_out, expand_in, expand_out, adapter_down, adapter_back, adapter_keys, adapter_values, adapter_rates, adapter_expand, adapter_mixer, adapter_hidden):
    weights = (norm_gains, head_gain, mixer_in.astype(jnp.float32), rate_in.astype(jnp.float32), kernel_taps.astype(jnp.float32), decay_scale, decay_bias, mixer_out.astype(jnp.float32), expand_in.astype(jnp.float32), expand_out.astype(jnp.float32))
    tables = tuple((table.astype(jnp.float32) for table in (adapter_down, adapter_back, adapter_keys, adapter_values, adapter_rates, adapter_expand, adapter_mixer, adapter_hidden)))

    def one_sequence(totals, inputs):
        resid, cotangent, labels, pick = inputs

        def apply_layer(value, held):
            return forward(value, held, weights, labels, pick)
        result, pullback = jax.vjp(apply_layer, resid.astype(jnp.float32), tables)
        input_grad, table_grads = pullback(cotangent.astype(jnp.float32))
        totals = tuple((total + grad for total, grad in zip(totals, table_grads)))
        return (totals, (result.astype(jnp.bfloat16), input_grad))
    start = tuple((jnp.zeros_like(table) for table in tables))
    totals, results = lax.scan(one_sequence, start, (hidden_in, out_grad, segment_ids, adapter_pick))
    outputs, input_grads = results
    return (outputs, input_grads, totals[0], totals[1], totals[2], totals[3], totals[4], totals[5], totals[6], totals[7])
```

```python
import functools

import jax
import jax.numpy as jnp
from jax import lax
from jax.experimental import pallas as pl
from jax.experimental.pallas import tpu as pltpu
from jax.sharding import PartitionSpec as P

DK = 128
DV = 256
B = 128
f32 = jnp.float32
b16 = jnp.bfloat16
EXACT = lax.Precision.HIGHEST


def mm(a, b, ca=1, cb=0):
    return lax.dot_general(
        a.astype(b16), b.astype(b16), (((ca,), (cb,)), ((), ())), preferred_element_type=f32
    )


def mm3(a, b):
    ah, bh = a.astype(b16), b.astype(b16)
    al, bl = (a - ah.astype(f32)).astype(b16), (b - bh.astype(f32)).astype(b16)
    return mm(ah, bh) + (mm(ah, bl) + mm(al, bh))


def unit_inverse(coupling, row, col):
    base = 16
    same = (row // base) == (col // base)
    power = jnp.where(same, coupling, 0.0)
    result = jnp.where(row == col, 1.0, 0.0) - power
    for _ in range(3):
        power = mm3(power, power)
        result = result + mm3(result, power)
    size = base
    while size < B:
        joined = ((row // (2 * size)) == (col // (2 * size))) & ((row // size) != (col // size))
        cross = jnp.where(joined, coupling, 0.0)
        result = result - mm3(result, mm3(cross, result))
        size *= 2
    return result


def block_view(b, cols, rows):
    here = pl.ds(pl.multiple_of(b * B, B), B)
    row = lax.broadcasted_iota(jnp.int32, (B, B), 0)
    col = lax.broadcasted_iota(jnp.int32, (B, B), 1)
    cum_c, beta, lab_c, flag = (cols[here, i : i + 1] for i in range(4))
    cum_r, lab_r = rows[b, 0:1, :], rows[b, 1:2, :]
    linked = (lab_c == lab_r) & (row >= col)
    decay = jnp.where(linked, jnp.exp(jnp.where(linked, cum_c - cum_r, 0.0)), 0.0)
    carry = flag * jnp.exp(cum_c)
    last = cum_c[B - 1 : B]
    tail = jnp.where(lab_c == lab_c[B - 1 : B], jnp.exp(last - cum_c), 0.0)
    return here, row, col, beta, decay, carry, tail


def forward_kernel(count, cols, rows, q, k, v, out, inv, fresh, states, wk, tk):
    width = v.shape[1]

    def before(b, carry_none):
        here, row, col, beta, decay, carry, tail = block_view(b, cols, rows)
        key = k[here, :]
        strict = jnp.where(row > col, decay, 0.0)
        inverse = unit_inverse(beta * mm(key, key, 1, 1) * strict, row, col)
        inv[here, :] = inverse.astype(b16)
        wk[here, :] = mm(inverse, (beta * carry) * key).astype(b16)
        fresh[here, :] = mm(inverse, beta * v[here, :])
        tk[here, :] = (tail * key).astype(b16)
        return carry_none

    lax.fori_loop(0, count, before, 0, unroll=2)

    def chain(b, state):
        here = pl.ds(pl.multiple_of(b * B, B), B)
        at = pl.ds(pl.multiple_of(b * DK, DK), DK)
        low = state.astype(b16)
        states[at, :] = low
        now = fresh[here, :] - mm(wk[here, :], low)
        fresh[here, :] = now
        final = pl.ds(b * B + B - 1, 1)
        keep = cols[final, 3:4] * jnp.exp(cols[final, 0:1])
        return keep * state + mm(tk[here, :], now, 0, 0)

    lax.fori_loop(0, count, chain, jnp.zeros((DK, width), f32))

    def after(b, carry_none):
        here, row, col, beta, decay, carry, tail = block_view(b, cols, rows)
        query = q[here, :].astype(b16)
        at = pl.ds(pl.multiple_of(b * DK, DK), DK)
        scores = mm(query, k[here, :], 1, 1) * decay
        out[here, :] = carry * mm(query, states[at, :]) + mm(scores, fresh[here, :])
        return carry_none

    lax.fori_loop(0, count, after, 0, unroll=2)


def delta_forward(cols, rows, q, k, v):
    length, width = v.shape
    count = length // B
    return pl.pallas_call(
        functools.partial(forward_kernel, count),
        out_shape=(
            jax.ShapeDtypeStruct((length, width), f32),
            jax.ShapeDtypeStruct((length, B), b16),
            jax.ShapeDtypeStruct((length, width), f32),
            jax.ShapeDtypeStruct((count * DK, width), b16),
        ),
        scratch_shapes=[pltpu.VMEM((length, DK), b16), pltpu.VMEM((length, DK), b16)],
        name="delta_forward",
    )(cols, rows, q, k, v)


def backward_kernel(
    count, cols, rows, q, k, v, dout, inv, fresh, states,
    dq, dk, dv, dcol, drow, wk, tk, dfresh, dstart, dends,
):
    width = v.shape[1]

    def before(b, carry_none):
        here, row, col, beta, decay, carry, tail = block_view(b, cols, rows)
        at = pl.ds(pl.multiple_of(b * DK, DK), DK)
        key, query, grad = k[here, :], q[here, :], dout[here, :]
        scores = mm(query, key, 1, 1) * decay
        wk[here, :] = mm(inv[here, :], (beta * carry) * key).astype(b16)
        tk[here, :] = (tail * key).astype(b16)
        dfresh[here, :] = mm(scores, grad, 0, 0)
        dstart[at, :] = mm(query, carry * grad, 0, 0)
        return carry_none

    lax.fori_loop(0, count, before, 0, unroll=2)

    def chain(step, dstate):
        b = count - 1 - step
        here = pl.ds(pl.multiple_of(b * B, B), B)
        at = pl.ds(pl.multiple_of(b * DK, DK), DK)
        low = dstate.astype(b16)
        dends[at, :] = low
        now = dfresh[here, :] + mm(tk[here, :], low)
        dfresh[here, :] = now
        final = pl.ds(b * B + B - 1, 1)
        keep = cols[final, 3:4] * jnp.exp(cols[final, 0:1])
        return keep * dstate + dstart[at, :] - mm(wk[here, :], now, 0, 0)

    lax.fori_loop(0, count, chain, jnp.zeros((DK, width), f32))

    def after(b, carry_none):
        here, row, col, beta, decay, carry, tail = block_view(b, cols, rows)
        at = pl.ds(pl.multiple_of(b * DK, DK), DK)
        key, query, grad = k[here, :], q[here, :], dout[here, :]
        key_low, query_low, grad_low = key.astype(b16), query.astype(b16), grad.astype(b16)
        state, dend = states[at, :], dends[at, :]
        new, value = fresh[here, :], v[here, :]
        new_low = new.astype(b16)
        strict = jnp.where(row > col, decay, 0.0)
        dright = mm(inv[here, :], dfresh[here, :], 0, 0)
        key_state = mm(key_low, state)
        query_state = mm(query_low, state)
        left = value - carry * key_state
        dv[here, :] = beta * dright
        dbeta = jnp.sum(dright * left, axis=1, keepdims=True)
        dcarry = jnp.sum(grad * query_state - (beta * dright) * key_state, axis=1, keepdims=True)
        moved = mm(new_low, dend, 1, 1)
        kk = mm(key_low, key_low, 1, 1)
        scores = mm(query_low, key_low, 1, 1) * decay
        dscores = mm(grad_low, new_low, 1, 1)
        dcoupling = -mm(dright, new_low, 1, 1)
        kk_decay = kk * strict
        dbeta = dbeta + jnp.sum(dcoupling * kk_decay, axis=1, keepdims=True)
        dqk = dscores * decay
        dkk = beta * dcoupling * strict
        dq[here, :] = mm(carry * grad, state, 1, 1) + mm(dqk, key_low)
        dkey = mm(-(beta * carry) * dright, state, 1, 1) + tail * moved
        dkey = dkey + mm(dqk, query_low, 0, 0) + mm(dkk, key_low) + mm(dkk, key_low, 0, 0)
        dk[here, :] = dkey
        spread = dscores * scores + dcoupling * (beta * kk_decay)
        dtail = tail * jnp.sum(key * moved, axis=1, keepdims=True)
        product = state.astype(f32) * dend.astype(f32)
        dkeep = jnp.sum(jnp.sum(product, axis=1, keepdims=True), axis=0, keepdims=True)
        place = lax.broadcasted_iota(jnp.int32, (B, 1), 0)
        extra = jnp.sum(dtail, axis=0, keepdims=True) + dkeep * carry[B - 1 : B]
        dcum = jnp.sum(spread, axis=1, keepdims=True) + dcarry * carry - dtail
        dcum = dcum + jnp.where(place == B - 1, extra, 0.0)
        lane = lax.broadcasted_iota(jnp.int32, (B, 8), 1)
        dcol[here, :] = jnp.where(lane == 0, dcum, jnp.where(lane == 1, dbeta, 0.0))
        minus = -jnp.sum(spread, axis=0, keepdims=True)
        sub = lax.broadcasted_iota(jnp.int32, (8, B), 0)
        drow[b, :, :] = jnp.where(sub == 0, minus, 0.0)
        return carry_none

    lax.fori_loop(0, count, after, 0, unroll=2)


def delta_backward(cols, rows, q, k, v, dout, inv, fresh, states):
    length, width = v.shape
    count = length // B
    return pl.pallas_call(
        functools.partial(backward_kernel, count),
        out_shape=(
            jax.ShapeDtypeStruct((length, DK), f32),
            jax.ShapeDtypeStruct((length, DK), f32),
            jax.ShapeDtypeStruct((length, width), f32),
            jax.ShapeDtypeStruct((length, 8), f32),
            jax.ShapeDtypeStruct((count, 8, B), f32),
        ),
        scratch_shapes=[
            pltpu.VMEM((length, DK), b16),
            pltpu.VMEM((length, DK), b16),
            pltpu.VMEM((length, width), f32),
            pltpu.VMEM((count * DK, width), f32),
            pltpu.VMEM((count * DK, width), b16),
        ],
        name="delta_backward",
    )(cols, rows, q, k, v, dout, inv, fresh, states)


def dot(a, b, ca=1, cb=0):
    return lax.dot_general(a, b, (((ca,), (cb,)), ((), ())), preferred_element_type=f32)


def unit_rows(value):
    return value * lax.rsqrt(jnp.sum(value * value, axis=-1, keepdims=True) + 1e-06)


def swish(value):
    return value * jax.nn.sigmoid(value)


def exchange_sum(value, axis):
    return jnp.sum(lax.all_gather(value, axis, axis=0), axis=0)


def gather_all(value):
    nc, nt = lax.axis_size("ctx"), lax.axis_size("tensor")
    piece, width = value.shape
    whole = lax.all_gather(value, ("ctx", "tensor"), axis=0)
    whole = whole.reshape(nc, nt, piece, width)
    return jnp.moveaxis(whole, 1, 2).reshape(nc * piece, nt * width)


def swap(value, axis, bit):
    n = lax.axis_size(axis)
    return lax.ppermute(value, axis, [(i, i ^ bit) for i in range(n)])


def scatter_all(part):
    me = lax.axis_index("tensor")
    core, side = lax.rem(me, 2), me // 2
    far = [part(2 * s + 1 - core).astype(b16) for s in (1 - side, side)]
    got = [swap(piece, "tensor", 1) for piece in far]
    away = (part(2 * (1 - side) + core) + got[0].astype(f32)).astype(b16)
    other = swap(away, "tensor", 2)
    here = part(2 * side + core) + got[1].astype(f32)
    mine = (here + other.astype(f32)).astype(b16)
    spread = lax.all_to_all(mine, "ctx", 0, 0, tiled=True)
    return jnp.sum(spread.astype(f32), axis=0)


def local(
    hidden_in, out_grad, segment_ids, adapter_pick, norm_gains, head_gain, mixer_in, rate_in,
    kernel_taps, decay_scale, decay_bias, mixer_out, expand_in, expand_out, adapter_down,
    adapter_back, adapter_keys, adapter_values, adapter_rates, adapter_expand, adapter_mixer,
    adapter_hidden,
):
    nc, nt = lax.axis_size("ctx"), lax.axis_size("tensor")
    me_c, me_t = lax.axis_index("ctx"), lax.axis_index("tensor")
    piece, width = hidden_in.shape[1:]
    length, model = nc * piece, nt * width
    block_d, heads = mixer_in.shape[:2]
    parts = nc // heads
    vp = DV // parts
    head, part = me_c // parts, lax.rem(me_c, parts)
    rank = adapter_keys.shape[2]
    adapters = adapter_keys.shape[0]
    units = expand_in.shape[2] // nc
    count = length // B
    pick = adapter_pick[0]
    x_here, g_here = hidden_in[0], out_grad[0]
    labels = segment_ids[0]

    def chosen(table):
        return lax.dynamic_index_in_dim(table, pick, 0, keepdims=False)

    def piece_of(array, start, size, axis):
        return lax.dynamic_slice_in_dim(array, start, size, axis)

    down, back = chosen(adapter_down), chosen(adapter_back)
    down_t = down.T
    mix_rank = 6 * rank
    by_part = mixer_in[..., 2 * DK :].reshape(block_d, heads, 2, parts, vp)
    qk = jnp.broadcast_to(mixer_in[:, :, None, : 2 * DK], (block_d, heads, parts, 2 * DK))
    low_in = jnp.broadcast_to(
        down_t[:, None, None, :mix_rank], (block_d, heads, parts, mix_rank)
    )
    rate_cols = jnp.broadcast_to(rate_in[:, :, None, :], (block_d, heads, parts, 2))
    filler = jnp.zeros((block_d, heads, parts, 128 - mix_rank - 2), b16)
    send_in = jnp.concatenate(
        [qk, by_part[:, :, 0], by_part[:, :, 1], low_in, rate_cols, filler], axis=-1
    )
    cols_in = send_in.shape[-1]
    send_in = jnp.moveaxis(send_in.reshape(block_d, nc, cols_in), 1, 0)
    w_in = lax.all_to_all(send_in, "ctx", 0, 0, tiled=True).reshape(model, cols_in)
    up = expand_in.reshape(block_d, 2, nc, units)
    up = jnp.moveaxis(up, 2, 0).reshape(nc, block_d, 2 * units)
    low_up = jnp.broadcast_to(down_t[None, :, mix_rank:], (nc, block_d, 2 * rank))
    w_up = lax.all_to_all(jnp.concatenate([up, low_up], axis=-1), "ctx", 0, 0, tiled=True)
    w_up = w_up.reshape(model, 2 * units + 2 * rank)
    dn = expand_out.reshape(nc, units, block_d)
    low_dn = jnp.broadcast_to(back[None], (nc, 2 * rank, block_d))
    w_dn = lax.all_to_all(jnp.concatenate([dn, low_dn], axis=1), "ctx", 0, 0, tiled=True)
    w_dn = jnp.moveaxis(w_dn, 0, 1).reshape(units + 2 * rank, model)
    back_out = w_dn[units : units + rank]
    w_dn = jnp.concatenate([w_dn[:units], w_dn[units + rank :]], axis=0)
    w_out = lax.all_gather(mixer_out, "ctx", axis=2, tiled=True).reshape(heads * DV, model)

    keys_here = piece_of(chosen(adapter_keys), head * DK, DK, 2)
    values_here = piece_of(chosen(adapter_values), head * DV + part * vp, vp, 2)
    rates_here = piece_of(chosen(adapter_rates), head, 1, 2)
    expand_here = piece_of(chosen(adapter_expand), me_c * units, units, 2)
    hidden_here = piece_of(chosen(adapter_hidden), me_c * units, units, 1)
    mixer_sel = chosen(adapter_mixer)

    def widen(factors):
        total = sum(f.shape[1] for f in factors)
        lines, at = [], 0
        for f in factors:
            lines.append(jnp.pad(f, ((0, 0), (at, total - at - f.shape[1]))))
            at += f.shape[1]
        return jnp.concatenate(lines, axis=0)

    lift = widen(
        [keys_here[0], keys_here[1], values_here[0], values_here[1], rates_here[0], rates_here[1]]
    )
    lift_up = widen([expand_here[0], expand_here[1]])

    x_all = gather_all(x_here)
    x_wide = x_all.astype(f32)
    r_first = lax.rsqrt(jnp.mean(x_wide * x_wide, axis=-1, keepdims=True) + 1e-06)
    first_norm = (x_wide * r_first * norm_gains[0]).astype(b16)
    base = dot(first_norm, w_in)
    inner = 2 * DK + vp
    outer = inner + vp
    low_mix = base[:, outer : outer + mix_rank].astype(b16)
    added = dot(low_mix, lift)
    pre = (base[:, :inner] + added[:, :inner]).astype(b16)
    gate = base[:, inner:outer] + added[:, inner:outer]
    rates = base[:, outer + mix_rank : outer + mix_rank + 2] + added[:, outer:]

    tap_all = piece_of(kernel_taps, head, 1, 1)[:, 0].astype(f32)
    taps = jnp.concatenate(
        [tap_all[:, : 2 * DK], piece_of(tap_all, 2 * DK + part * vp, vp, 1)], axis=1
    )
    scale_here, bias_here = piece_of(decay_scale, head, 1, 0), piece_of(decay_bias, head, 1, 0)
    reach = taps.shape[0]
    keeps = []
    for back_by in range(1, reach):
        earlier = jnp.concatenate([jnp.full((back_by,), -1, jnp.int32), labels[:-back_by]])
        keeps.append(jnp.where(earlier == labels, 1.0, 0.0)[:, None])
    lower = jnp.tril(jnp.ones((B, B), f32))

    def prepare(pre_in, rates_in):
        mixed_in = taps[0] * pre_in
        for back_by in range(1, reach):
            moved = jnp.pad(pre_in[:-back_by], ((back_by, 0), (0, 0)))
            mixed_in = mixed_in + taps[back_by] * moved * keeps[back_by - 1]
        active = swish(mixed_in)
        query = unit_rows(active[:, :DK]) * DK ** (-0.5)
        key = unit_rows(active[:, DK : 2 * DK])
        beta = jax.nn.sigmoid(rates_in[:, 1])
        log_decay = -scale_here * jax.nn.softplus(rates_in[:, 0] + bias_here)
        cum = dot_exact(log_decay.reshape(count, B), lower)
        return query, key, active[:, 2 * DK :], beta, cum.reshape(length)

    def dot_exact(a, tri):
        return jnp.einsum("bj,ij->bi", a, tri, precision=EXACT)

    (query, key, value, beta, cum), prepare_back = jax.vjp(prepare, pre.astype(f32), rates)
    label_f = labels.astype(f32)
    by_block = labels.reshape(count, B)
    before = jnp.concatenate([jnp.full((1,), -1, jnp.int32), by_block[:-1, -1]])
    flag = jnp.where(by_block == before[:, None], 1.0, 0.0).reshape(length)
    nil = jnp.zeros_like(cum)
    cols = jnp.stack([cum, beta, label_f, flag, nil, nil, nil, nil], axis=1)
    row_nil = jnp.zeros((count, 6, B), f32)
    rows = jnp.concatenate(
        [cum.reshape(count, 1, B), label_f.reshape(count, 1, B), row_nil], axis=1
    )
    mixed, inv, fresh, states = delta_forward(cols, rows, query, key, value)

    def over_parts(stat):
        total = stat
        for step in range(1, parts):
            pairs = [(i, (i // parts) * parts + (i % parts + step) % parts) for i in range(nc)]
            total = total + lax.ppermute(stat, "ctx", pairs)
        return total

    gain_here = piece_of(head_gain, part * vp, vp, 0)
    square = over_parts(jnp.sum(mixed * mixed, axis=-1).reshape(count, B)).reshape(length, 1)
    r_head = lax.rsqrt(square / DV + 1e-05)
    gate_sig = jax.nn.sigmoid(gate)
    gate_act = gate * gate_sig
    attended = (mixed * r_head * gain_here * gate_act).astype(b16)

    att_t = lax.all_to_all(attended.reshape(nc, piece, vp), "ctx", 0, 0, tiled=True)
    att_t = jnp.moveaxis(att_t, 0, 1).reshape(piece, nc * vp)
    low_out = dot(att_t, mixer_sel, 1, 1).astype(b16)
    branch = (dot(att_t, w_out) + dot(low_out, back_out)).astype(b16)
    branch = jnp.moveaxis(branch.reshape(piece, nt, width), 1, 0)
    branch = lax.all_to_all(branch, "tensor", 0, 0, tiled=True)
    x_own = x_here.astype(f32)
    resid_mid = x_own + jnp.sum(branch.astype(f32), axis=0)
    gains = piece_of(norm_gains, me_t * width, width, 1)
    r_second = lax.rsqrt(
        exchange_sum(jnp.sum(resid_mid * resid_mid, axis=-1), "tensor") / model + 1e-06
    )[:, None]
    second_here = (resid_mid * r_second * gains[1]).astype(b16)

    second_norm = gather_all(second_here)
    g_all = gather_all(g_here)
    up_all = dot(second_norm, w_up)
    low_ffn = up_all[:, 2 * units :].astype(b16)
    gate_up = up_all[:, : 2 * units] + dot(low_ffn, lift_up)
    gate_f, up_f = gate_up[:, :units], gate_up[:, units:]
    sig_f = jax.nn.sigmoid(gate_f)
    silu_f = gate_f * sig_f
    hidden_act = (silu_f * up_f).astype(b16)
    low_hid = dot(hidden_act, hidden_here, 1, 1).astype(b16)
    d_hid_all = dot(g_all, w_dn, 1, 1)
    d_low_hid = d_hid_all[:, units:].astype(b16)
    d_hid = d_hid_all[:, :units] + dot(d_low_hid, hidden_here)
    d_gate = sig_f * (1.0 + gate_f * (1.0 - sig_f)) * up_f * d_hid
    d_up = silu_f * d_hid
    d_gate_up = jnp.concatenate([d_gate, d_up], axis=1).astype(b16)
    d_low_ffn = dot(d_gate_up, lift_up, 1, 1).astype(b16)
    d_up_all = jnp.concatenate([d_gate_up, d_low_ffn], axis=1)
    hid_all = jnp.concatenate([hidden_act, low_hid], axis=1)

    def second_part(t):
        rows_t = piece_of(w_up, t * width, width, 0)
        return dot(d_up_all, rows_t, 1, 1).reshape(nc, piece, width)

    def out_part(t):
        return dot(hid_all, piece_of(w_dn, t * width, width, 1)).reshape(nc, piece, width)

    d_second = scatter_all(second_part)
    out_share = scatter_all(out_part)
    hidden_out = (resid_mid + out_share).astype(b16)

    def rms_back(grad, gain, value, r):
        w = grad * gain
        mean = exchange_sum(jnp.sum(value * w, axis=-1), "tensor")[:, None] / model
        return r * w - r * r * r * value * mean

    d_mid = g_here.astype(f32) + rms_back(d_second, gains[1], resid_mid, r_second)
    d_branch = lax.all_gather(d_mid.astype(b16), "tensor", axis=1, tiled=True)
    d_low_out = dot(d_branch, back_out, 1, 1).astype(b16)
    d_att = dot(d_branch, w_out, 1, 1) + dot(d_low_out, mixer_sel)
    d_mix_part = dot(d_low_out, att_t, 0, 0)
    d_att = jnp.concatenate([d_att, d_mix_part], axis=0).astype(b16)
    d_att = jnp.moveaxis(d_att.reshape(piece + rank, nc, vp), 1, 0)
    d_att = lax.all_to_all(d_att, "ctx", 0, 0, tiled=True)
    grad_mixer = jnp.sum(d_att[:, piece:].astype(f32), axis=0)
    d_att = d_att[:, :piece].astype(f32).reshape(length, vp)

    d_normed = d_att * gain_here * gate_act
    d_out_gate = d_att * (mixed * r_head * gain_here)
    d_out_gate = (d_out_gate * gate_sig * (1.0 + gate * (1.0 - gate_sig))).astype(b16)
    stat = over_parts(jnp.sum(mixed * d_normed, axis=-1).reshape(count, B)).reshape(length, 1)
    d_mixed = r_head * d_normed - r_head * r_head * r_head * mixed * (stat / DV)
    dq, dk, dv, dcol, drow = delta_backward(
        cols, rows, query, key, value, d_mixed, inv, fresh, states
    )
    d_cum = dcol[:, 0] + drow[:, 0].reshape(length)
    d_pre, d_rates = prepare_back((dq, dk, dv, dcol[:, 1], d_cum))
    d_cols = jnp.concatenate([d_pre.astype(b16), d_out_gate, d_rates.astype(b16)], axis=1)
    d_low_mix = dot(d_cols, lift, 1, 1).astype(b16)
    zero_cols = jnp.zeros((length, cols_in - outer - mix_rank - 2), b16)
    d_all = jnp.concatenate(
        [d_cols[:, :outer], d_low_mix, d_cols[:, outer:], zero_cols], axis=1
    )

    g_rows = jnp.concatenate(
        [
            dot(d_low_mix, first_norm, 0, 0),
            dot(d_low_ffn, second_norm, 0, 0),
            dot(low_out, d_branch, 0, 0),
            dot(low_hid, g_all, 0, 0),
        ],
        axis=0,
    )
    n_rows = g_rows.shape[0]
    thin = model // (nc * nt)
    g_rows = jnp.transpose(g_rows.reshape(n_rows, nc, nt, thin), (2, 1, 0, 3))
    g_rows = g_rows.reshape(nt, nc, n_rows * thin // width, width)
    spare = (-g_rows.shape[2]) % 16
    g_rows = jnp.pad(g_rows, ((0, 0), (0, 0), (0, spare), (0, 0)))

    def first_part(t):
        rows_t = piece_of(w_in, t * width, width, 0)
        share = dot(d_all, rows_t, 1, 1).reshape(nc, piece, width)
        return jnp.concatenate([share, lax.dynamic_index_in_dim(g_rows, t, 0, False)], axis=1)

    summed = scatter_all(first_part)
    d_first = summed[:piece]
    r_own = piece_of(r_first, me_c * piece, piece, 0)
    input_grad = d_mid + rms_back(d_first, gains[0], x_own, r_own)
    thin_grads = summed[piece : piece + n_rows * thin // width].reshape(n_rows, thin)

    ranks = [low_mix[:, i * rank : (i + 1) * rank] for i in range(6)]
    g_keys = [dot(ranks[i], d_cols[:, i * DK : (i + 1) * DK], 0, 0) for i in range(2)]
    g_values = [
        dot(ranks[2 + i], d_cols[:, 2 * DK + i * vp : 2 * DK + (i + 1) * vp], 0, 0)
        for i in range(2)
    ]
    g_rates = [dot(ranks[4 + i], d_cols[:, outer + i : outer + i + 1], 0, 0) for i in range(2)]
    g_expand = [
        dot(low_ffn[:, i * rank : (i + 1) * rank], d_gate_up[:, i * units : (i + 1) * units], 0, 0)
        for i in range(2)
    ]
    g_hidden = dot(d_low_hid, hidden_act, 0, 0)
    wide = jnp.concatenate(
        g_keys + g_values + [grad_mixer] + g_expand + [g_hidden] + g_rates, axis=1
    )
    wide = jnp.pad(wide, ((0, 0), (0, (-wide.shape[1]) % 128))).astype(b16)
    wide_all = lax.all_gather(wide, "ctx", axis=0).astype(f32)

    def spread(grad):
        at = lax.broadcasted_iota(jnp.int32, (adapters,) + (1,) * grad.ndim, 0)
        return jnp.where(at == pick, grad[None], 0.0)

    def by_head(start, size):
        got = wide_all[:, :, start : start + size].reshape(heads, parts, rank, size)
        return jnp.moveaxis(jnp.sum(got, axis=1), 0, 1).reshape(rank, heads * size)

    def by_device(start, size):
        got = wide_all[:, :, start : start + size]
        return jnp.moveaxis(got, 0, 1).reshape(rank, nc * size)

    at = 2 * DK
    out_keys = jnp.stack([by_head(0, DK), by_head(DK, DK)])
    out_values = jnp.stack([by_device(at, vp), by_device(at + vp, vp)])
    out_mixer = by_device(at + 2 * vp, vp)
    at += 3 * vp
    out_expand = jnp.stack([by_device(at, units), by_device(at + units, units)])
    out_hidden = by_device(at + 2 * units, units)
    at += 3 * units
    out_rates = jnp.stack([by_head(at, 1), by_head(at + 1, 1)])
    return (
        hidden_out[None],
        input_grad[None],
        spread(thin_grads[: 8 * rank]),
        spread(thin_grads[8 * rank :]),
        spread(out_keys),
        spread(out_values),
        spread(out_rates),
        spread(out_expand),
        spread(out_mixer),
        spread(out_hidden),
    )


def solution(mesh):
    in_specs = (
        P(None, "ctx", "tensor"),
        P(None, "ctx", "tensor"),
        P(),
        P(),
        P(),
        P(),
        P("ctx", "tensor", None),
        P("ctx", "tensor", None),
        P(None, "tensor", None),
        P("tensor"),
        P("tensor"),
        P("tensor", None, "ctx"),
        P("ctx", None, "tensor"),
        P("tensor", "ctx"),
        P(None, None, "ctx"),
        P(None, None, "ctx"),
        P(None, None, None, "tensor"),
        P(None, None, None, "tensor"),
        P(None, None, None, "tensor"),
        P(None, None, None, "tensor"),
        P(None, None, "tensor"),
        P(None, None, "tensor"),
    )
    out_specs = (
        P(None, "ctx", "tensor"),
        P(None, "ctx", "tensor"),
        P(None, None, ("ctx", "tensor")),
        P(None, None, ("ctx", "tensor")),
        P(None, None, None, "tensor"),
        P(None, None, None, "tensor"),
        P(None, None, None, "tensor"),
        P(None, None, None, "tensor"),
        P(None, None, "tensor"),
        P(None, None, "tensor"),
    )
    return jax.shard_map(local, mesh=mesh, in_specs=in_specs, out_specs=out_specs, check_vma=False)
```
